256 devices in a mesh: pipe: 8 (over y, x_lo), ctx: 32 (over z, x_hi, core).
Axes of the slice: x: 4 (x_hi: 2, x_lo: 2; x = x_hi * 2 + x_lo), y: 4, z: 8, core: 2. Of those that a mesh axis runs over, the one named last changes fastest.
Arguments:
- queries: bfloat16 [8, 8192, 2048], P('pipe', 'ctx'), may hold values from -70 to 70
- key_rows: bfloat16 [8, 8192, 512], P('pipe', 'ctx'), may hold values from -6 to 6
- value_rows: bfloat16 [8, 8192, 512], P('pipe', 'ctx'), may hold values from -6 to 6
- out_grad: bfloat16 [8, 8192, 2048], P('pipe', 'ctx'), may hold values from -6 to 6
- doc_blocks: int32 [8, 64], P('pipe'), may hold values from 0 to 15, never falling along the last dimension, each value on 1 to 8 neighbouring positions
Outputs:
- attn_out: bfloat16 [8, 8192, 2048], P('pipe', 'ctx')
- grad_query: bfloat16 [8, 8192, 2048], P('pipe', 'ctx')
- grad_key: bfloat16 [8, 8192, 512], P('pipe', 'ctx')
- grad_value: bfloat16 [8, 8192, 512], P('pipe', 'ctx')
The draws below stay inside these ranges and needn't reach their ends.
Inputs may be any that keep to these rules, and one draw needn't show every extreme that they name: `doc_blocks`: each document is a run of 1 to 8 consecutive blocks; ids never fall along a section's sequence, and in each section some document has exactly 8 blocks.
All inputs are finite; a program needn't handle non-finite values.
Results may differ from the reference program's by a relative error of at most 0.014.
Values may be sent and summed in bfloat16 or wider, within the bound.
A program may use at most 64 MiB of HBM per device.

```python
import math
import jax
import jax.numpy as jnp
import numpy as np
from jax import lax

HD = 128
H = 16
KVH = 4
BLK = 128
MOST_BLK = 8
TOK_DEV = 256
SECTIONS = 8
SEQ = 8192
NBLK = 64
REACH = 4


def joint_draw(base_key):
    query_source = jax.random.fold_in(base_key, 101)
    key_source = jax.random.fold_in(base_key, 202)
    group_size = H // KVH
    query_shape = (SECTIONS, SEQ, KVH, group_size, HD)
    key_shape = (SECTIONS, SEQ, KVH, HD)
    query_draw = jax.random.truncated_normal(query_source, -6.0, 6.0, query_shape, jnp.float32)
    key_draw = jax.random.truncated_normal(key_source, -6.0, 6.0, key_shape, jnp.float32)
    return (query_draw.reshape(SECTIONS, SEQ, H * HD), key_draw.reshape(SECTIONS, SEQ, KVH * HD))


def draw_queries(key, part):
    return joint_draw(key)[0].astype(jnp.bfloat16)


def draw_key_rows(key, part):
    return joint_draw(key)[1].astype(jnp.bfloat16)


def block_levels(own_key, extent, shards, least, top_value):
    level, own = 1.0, jax.random.fold_in(own_key, 6)
    for position, shards_of in shards:
        draws = jnp.exp(jax.random.uniform(jax.random.fold_in(own, position), (shards_of,), jnp.float32, least / len(shards), top_value / len(shards)))
        level = level * jnp.repeat(draws, extent[position] // shards_of).reshape([-1 if axis == position else 1 for axis in range(len(extent))])
    return level


def profile(number_of, total, limit, lean):
    weights = [(1 << 20) // math.isqrt(standing ** lean) + 1 for standing in range(2, number_of + 1)]
    spare, holding = total - limit - (number_of - 1), [1] * (number_of - 1)
    while spare > 0:
        movable = [i for i in range(number_of - 1) if holding[i] < limit]
        whole, budget = sum([weights[i] for i in movable]), spare
        for i in movable:
            more = min(limit - holding[i], max(1, budget * weights[i] // whole), spare)
            holding[i] = holding[i] + more
            spare = spare - more
    return np.array([limit] + holding)


def uneven_parts(own_key, amount, total, reach, lean):
    if amount == 2:
        one = jax.random.randint(own_key, (), max(1, total - reach), min(reach, total - 1) + 1)
        return jnp.stack([one, total - one])
    tallies = jnp.asarray(profile(amount, total, reach, lean), jnp.int32)
    couples = (amount - 1) // 2
    donor, receiver = tallies[1:1 + 2 * couples:2], tallies[2:2 + 2 * couples:2]
    slack = jnp.minimum(donor - 1, reach - receiver)
    passed = jax.random.randint(jax.random.fold_in(own_key, 1), (couples,), 0, 1 << 20) % (slack + 1)
    tallies = tallies.at[1:1 + 2 * couples:2].set(donor - passed).at[2:2 + 2 * couples:2].set(receiver + passed)
    return tallies[jax.random.permutation(jax.random.fold_in(own_key, 2), amount)]


def scatter_about(rng, shape, deviation, most, pieces=(), held_as=jnp.bfloat16):
    factor_of = block_levels(rng, shape, pieces, -0.22, 0.18) if pieces else 1.0
    array = jax.random.normal(rng, shape, jnp.float32) * deviation * factor_of
    return jnp.minimum(jnp.maximum(array, -most), most).astype(held_as)


def setup_inputs(seed: int = 0) -> dict:
    seeds = jax.random.split(jax.random.key(seed), 6)
    queries = draw_queries(jax.random.fold_in(seeds[5], 71), 0)
    key_rows = draw_key_rows(jax.random.fold_in(seeds[5], 71), 0)
    value_rows = scatter_about(seeds[2], (SECTIONS, SEQ, KVH * HD), 1.0, 6.0, ((0, 8), (1, 32)))
    out_grad = scatter_about(seeds[3], (SECTIONS, SEQ, H * HD), 1.0, 6.0, ((0, 8), (1, 32)))
    doc_blocks = jax.vmap(lambda own: jnp.searchsorted(jnp.cumsum(uneven_parts(own, NBLK // 4, NBLK, MOST_BLK, 1)), jnp.arange(NBLK), side="right"))(jax.random.split(seeds[4], SECTIONS)).reshape((SECTIONS, NBLK)).astype(jnp.int32)
    return dict(queries=queries, key_rows=key_rows, value_rows=value_rows, out_grad=out_grad, doc_blocks=doc_blocks)


def low_round(values_in):
    return lax.optimization_barrier(values_in.astype(jnp.bfloat16)).astype(jnp.float32)

def one_section(inputs):
    queries, key_rows, value_rows, out_grad, doc_row = inputs
    group_size = H // KVH
    window = MOST_BLK * BLK
    block_count = SEQ // BLK
    score_scale = 1.0 / math.sqrt(HD)
    query_full = queries.astype(jnp.float32).reshape(SEQ, KVH, group_size, HD)
    grad_full = out_grad.astype(jnp.float32).reshape(SEQ, KVH, group_size, HD)
    key_full = key_rows.astype(jnp.float32).reshape(SEQ, KVH, HD)
    value_full = value_rows.astype(jnp.float32).reshape(SEQ, KVH, HD)
    pad_rows = window - BLK
    key_pad = jnp.concatenate([jnp.zeros((pad_rows, KVH, HD), jnp.float32), key_full], 0)
    value_pad = jnp.concatenate([jnp.zeros((pad_rows, KVH, HD), jnp.float32), value_full], 0)
    doc_front = jnp.concatenate([jnp.full((MOST_BLK - 1,), -1, jnp.int32), doc_row.astype(jnp.int32)], 0)

    def query_block(block):
        offset = (block * BLK).astype(jnp.int32)
        query_here = lax.dynamic_slice_in_dim(query_full, offset, BLK, 0)
        grad_here = lax.dynamic_slice_in_dim(grad_full, offset, BLK, 0)
        key_window = lax.dynamic_slice_in_dim(key_pad, offset, window, 0)
        value_window = lax.dynamic_slice_in_dim(value_pad, offset, window, 0)
        key_doc = jnp.repeat(lax.dynamic_slice_in_dim(doc_front, block.astype(jnp.int32), MOST_BLK, 0), BLK)
        key_pos = offset - pad_rows + jnp.arange(window, dtype=jnp.int32)
        query_pos = offset + jnp.arange(BLK, dtype=jnp.int32)
        query_doc = lax.dynamic_slice_in_dim(doc_row.astype(jnp.int32), block.astype(jnp.int32), 1, 0)[0]
        visible = (key_doc[None, :] == query_doc) & (key_pos[None, :] <= query_pos[:, None])
        scores = jnp.einsum('tgcd,kgd->gctk', query_here, key_window) * score_scale
        masked = jnp.where(visible, scores, -1e+30)
        maxima = lax.optimization_barrier(jnp.max(masked, axis=-1))
        totals = lax.optimization_barrier(jnp.sum(jnp.where(visible, jnp.exp(masked - maxima[..., None]), 0.0), axis=-1))
        log_norm = maxima + jnp.log(totals)
        probs = jnp.where(visible, jnp.exp(scores - log_norm[..., None]), 0.0)
        probs_low = low_round(probs)
        output = jnp.einsum('gctk,kgd->tgcd', probs_low, value_window)
        out_low = output.astype(jnp.bfloat16)
        row_dots = jnp.einsum('tgcd,tgcd->gct', grad_here, lax.optimization_barrier(out_low).astype(jnp.float32))
        prob_grad = jnp.einsum('tgcd,kgd->gctk', grad_here, value_window)
        score_grad = low_round(probs * (prob_grad - row_dots[..., None]))
        query_grad = jnp.einsum('gctk,kgd->tgcd', score_grad, key_window) * score_scale
        return (out_low, query_grad.astype(jnp.bfloat16), log_norm, row_dots)
    out_blocks, query_blocks, norm_blocks, dot_blocks = lax.map(query_block, jnp.arange(block_count, dtype=jnp.int32))
    attn_out = out_blocks.reshape(SEQ, H * HD)
    query_grad = query_blocks.reshape(SEQ, H * HD)
    log_norm = norm_blocks.transpose(1, 2, 0, 3).reshape(KVH, group_size, SEQ)
    row_dots = dot_blocks.transpose(1, 2, 0, 3).reshape(KVH, group_size, SEQ)
    query_back = jnp.concatenate([query_full, jnp.zeros((pad_rows, KVH, group_size, HD), jnp.float32)], 0)
    grad_back = jnp.concatenate([grad_full, jnp.zeros((pad_rows, KVH, group_size, HD), jnp.float32)], 0)
    norm_back = jnp.concatenate([log_norm, jnp.zeros((KVH, group_size, pad_rows), jnp.float32)], 2)
    dots_back = jnp.concatenate([row_dots, jnp.zeros((KVH, group_size, pad_rows), jnp.float32)], 2)
    doc_back = jnp.concatenate([doc_row.astype(jnp.int32), jnp.full((MOST_BLK - 1,), -2, jnp.int32)], 0)

    def key_block(block):
        offset = (block * BLK).astype(jnp.int32)
        key_here = lax.dynamic_slice_in_dim(key_full, offset, BLK, 0)
        value_here = lax.dynamic_slice_in_dim(value_full, offset, BLK, 0)
        query_window = lax.dynamic_slice_in_dim(query_back, offset, window, 0)
        grad_window = lax.dynamic_slice_in_dim(grad_back, offset, window, 0)
        norm_window = lax.dynamic_slice_in_dim(norm_back, offset, window, 2)
        dots_window = lax.dynamic_slice_in_dim(dots_back, offset, window, 2)
        query_doc = jnp.repeat(lax.dynamic_slice_in_dim(doc_back, block.astype(jnp.int32), MOST_BLK, 0), BLK)
        key_doc = lax.dynamic_slice_in_dim(doc_row.astype(jnp.int32), block.astype(jnp.int32), 1, 0)[0]
        query_pos = offset + jnp.arange(window, dtype=jnp.int32)
        key_pos = offset + jnp.arange(BLK, dtype=jnp.int32)
        visible = (query_doc[:, None] == key_doc) & (key_pos[None, :] <= query_pos[:, None])
        scores = jnp.einsum('tgcd,kgd->gctk', query_window, key_here) * score_scale
        probs = jnp.where(visible, jnp.exp(scores - norm_window[..., None]), 0.0)
        probs_low = low_round(probs)
        prob_grad = jnp.einsum('tgcd,kgd->gctk', grad_window, value_here)
        score_grad = low_round(probs * (prob_grad - dots_window[..., None]))
        key_shard = offset // TOK_DEV
        query_shard = query_pos // TOK_DEV
        key_grad = jnp.zeros((BLK, KVH, HD), jnp.float32)
        value_grad = jnp.zeros((BLK, KVH, HD), jnp.float32)
        for distance in range(REACH + 1):
            pick = (query_shard == key_shard + distance)[None, None, :, None]
            key_term = jnp.einsum('gctk,tgcd->kgd', jnp.where(pick, score_grad, 0.0), query_window) * score_scale
            value_term = jnp.einsum('gctk,tgcd->kgd', jnp.where(pick, probs_low, 0.0), grad_window)
            if distance > 0:
                key_term = low_round(key_term)
                value_term = low_round(value_term)
            key_grad = key_grad + key_term
            value_grad = value_grad + value_term
        return (key_grad.astype(jnp.bfloat16), value_grad.astype(jnp.bfloat16))
    key_blocks, value_blocks = lax.map(key_block, jnp.arange(block_count, dtype=jnp.int32))
    key_grad = key_blocks.reshape(SEQ, KVH * HD)
    value_grad = value_blocks.reshape(SEQ, KVH * HD)
    return (attn_out, query_grad, key_grad, value_grad)

def to_previous(stacked):
    return jnp.concatenate([stacked[1:], jnp.zeros_like(stacked[:1])], 0)

def reference(queries, key_rows, value_rows, out_grad, doc_blocks):
    attn_out, query_grad, key_grad, value_grad = lax.map(one_section, (queries, key_rows, value_rows, out_grad, doc_blocks))
    return (attn_out, to_previous(query_grad), to_previous(key_grad), to_previous(value_grad))
```

```python
import functools
import math

import jax
import jax.numpy as jnp
from jax import lax
from jax.experimental import pallas as pl
from jax.experimental.pallas import tpu as pltpu
from jax.sharding import PartitionSpec as P

MESH = pl.DeviceIdType.MESH
BF16 = jnp.bfloat16
F32 = jnp.float32
BLK = 128
SCALE = 1.0 / math.sqrt(128.0)
SCALE2 = SCALE * math.log2(math.e)
HIDE = 1e30
ROWS = 11 * BLK
WIN = 8 * BLK


def dot(a, b, dims):
    return lax.dot_general(a, b, (dims, ((), ())), preferred_element_type=F32)


def kernel(
    sections, shards,
    doc_ref, q_hbm, k_hbm, v_hbm, g_hbm,
    out_ref, gq_ref, gk_ref, gv_ref,
    qb_ref, gb_ref, kv_ref, kvt_ref, s_ref, dp_ref, e_ref, ds_ref, acc_ref, dgn_ref, q2_ref,
    o_st, dq_st, c2_st, c1_st, own_st, c2_rx, nxt_rx, own_rx,
    io_loc, io_snd, io_rcv, kv_loc, kv_snd, kv_rcv, o_sem, o_rcv, dq_snd, dq_rcv,
    c2_snd, c2_rcv, c1_snd, c1_rcv, own_snd, own_rcv,
):
    p = lax.axis_index("pipe")
    dev = lax.axis_index("ctx")
    core = lax.rem(dev, 2)
    chip = lax.div(dev, 2)
    chips = shards // 2
    nxt_p = lax.rem(p + 1, sections)
    prv_p = lax.rem(p + sections - 1, sections)

    def at(section, hop, which):
        return (section, 2 * lax.rem(chip + hop + chips, chips) + which)

    partner = (p, 2 * chip + 1 - core)
    barrier = pltpu.get_barrier_semaphore()
    sources = [partner, at(p, 2, core)]
    for which in range(2):
        sources += [at(p, -1, which), at(p, -2, which), at(nxt_p, 0, which), at(nxt_p, 1, which)]
    for source in sources:
        pl.semaphore_signal(barrier, inc=1, device_id=source, device_id_type=MESH)
    pl.semaphore_wait(barrier, len(sources))

    def remote(src, dst, snd, rcv, target):
        return pltpu.make_async_remote_copy(
            src_ref=src, dst_ref=dst, send_sem=snd, recv_sem=rcv,
            device_id=target, device_id_type=MESH,
        )

    def kv_cols(ref, rows, which, g):
        return ref.at[0, rows, pl.ds(pl.multiple_of((2 * which + g) * BLK, BLK), BLK)]

    kv_hbm = (k_hbm, v_hbm)
    io_hbm = (q_hbm, g_hbm)
    io_buf = (qb_ref, gb_ref)
    mine = pl.ds(pl.multiple_of(core * 256, 256), 256)
    whole = pl.ds(0, 256)

    def io_copies(g):
        copies = []
        for i in range(2):
            src = lambda which: io_hbm[i].at[0, :, pl.ds(pl.multiple_of(which * 1024 + g * 512, 512), 512)]
            dst = io_buf[i].at[g, mine, :]
            copies.append(pltpu.make_async_copy(src(core), dst, io_loc.at[g, i]))
            copies.append(remote(src(1 - core), dst, io_snd.at[g, i], io_rcv.at[g, i], partner))
        return copies

    def kv_own(g):
        copies = []
        for i in range(2):
            dst = kv_ref.at[i, g, pl.ds(pl.multiple_of(896 + core * 256, 128), 256), :]
            copies.append(pltpu.make_async_copy(kv_cols(kv_hbm[i], whole, core, g), dst, kv_loc.at[g, i]))
            copies.append(
                remote(kv_cols(kv_hbm[i], whole, 1 - core, g), dst, kv_snd.at[0, g, i], kv_rcv.at[0, g, i], partner)
            )
        return copies

    def kv_one(g):
        copies = []
        for which in range(2):
            for i in range(2):
                dst = kv_ref.at[i, g, pl.ds(pl.multiple_of(384 + core * 256, 128), 256), :]
                copies.append(
                    remote(
                        kv_cols(kv_hbm[i], whole, which, g), dst,
                        kv_snd.at[1 + which, g, i], kv_rcv.at[1 + core, g, i], at(p, 1, which),
                    )
                )
        return copies

    def kv_two(g, late):
        copies = []
        for which in range(2):
            for i in range(2):
                rows = pl.ds(128, 128) if late == 0 else whole
                to = pl.ds(0, 128) if late == 0 else pl.ds(128, 256)
                copies.append(
                    remote(
                        kv_cols(kv_hbm[i], rows, which, g), kv_ref.at[i, g, to, :],
                        kv_snd.at[3 + which, g, i], kv_rcv.at[3 + late, g, i], at(p, 2, which),
                    )
                )
        return copies

    for g in range(2):
        for copy in kv_one(g):
            copy.start()
        for late in range(2):
            @pl.when(core == late)
            def _():
                for copy in kv_two(g, late):
                    copy.start()
        for copy in kv_own(g) + io_copies(g):
            copy.start()

    acc_ref[...] = jnp.zeros_like(acc_ref)
    keep = jnp.where(p == 0, 0.0, 1.0).astype(F32)
    causal = lax.broadcasted_iota(jnp.int32, (BLK, 256), 0) <= lax.rem(
        lax.broadcasted_iota(jnp.int32, (BLK, 256), 1), BLK
    )

    def take_group(g):
        for i in range(2):
            pltpu.make_async_copy(io_buf[i].at[g, whole, :], io_buf[i].at[g, whole, :], io_loc.at[g, i]).wait()
            pltpu.make_async_copy(io_buf[i].at[g, whole, :], io_buf[i].at[g, whole, :], io_rcv.at[g, i]).wait()
            here = kv_ref.at[i, g, whole, :]
            half = kv_ref.at[i, g, pl.ds(0, 128), :]
            pltpu.make_async_copy(here, here, kv_loc.at[g, i]).wait()
            for source in (0, 1, 2, 4):
                pltpu.make_async_copy(here, here, kv_rcv.at[source, g, i]).wait()
            pltpu.make_async_copy(half, half, kv_rcv.at[3, g, i]).wait()
        for i in range(2):
            kvt_ref[i, g] = kv_ref[i, g].T

    def pair(g, qb, hp, hide):
        row = pl.multiple_of(qb * BLK, BLK)
        win = pl.ds(row, WIN)
        blk = pl.ds(row, BLK)
        cols = pl.ds(hp * 256, 256)
        lo, hi = slice(hp * 256, hp * 256 + 128), slice(hp * 256 + 128, hp * 256 + 256)
        q2 = jnp.concatenate([qb_ref[g, blk, lo], qb_ref[g, blk, hi]], 0)
        q2_ref[cols, :] = q2
        s_ref[hp] = dot(kv_ref[0, g, win, :], q2, ((1,), (1,)))
        top = None
        for kb in range(8):
            rows = slice(kb * BLK, (kb + 1) * BLK)
            tile = s_ref[hp, rows, :]
            if kb == 7:
                tile = jnp.where(causal, tile, -HIDE)
                s_ref[hp, rows, :] = tile
            high = jnp.max(tile, axis=0, keepdims=True)
            if kb < 7:
                high = high - hide[kb]
            top = high if top is None else jnp.maximum(top, high)
        top = top * SCALE2
        total = jnp.zeros((1, 256), F32)
        for kb in range(8):
            rows = slice(kb * BLK, (kb + 1) * BLK)
            off = top + hide[kb] if kb < 7 else top
            e = jnp.exp2(s_ref[hp, rows, :] * SCALE2 - off)
            total = total + jnp.sum(e, axis=0, keepdims=True)
            e_ref[rows, cols] = e.astype(BF16)
        inv = 1.0 / total
        ot = dot(kvt_ref[1, g, :, win], e_ref[:, cols], ((1,), (0,))) * inv
        o_st[g, blk, lo] = ot[:, :128].T.astype(BF16)
        o_st[g, blk, hi] = ot[:, 128:].T.astype(BF16)
        g2 = jnp.concatenate([gb_ref[g, blk, lo], gb_ref[g, blk, hi]], 0)
        gtn = (g2.astype(F32).T * inv).astype(BF16)
        rd = jnp.sum(ot.astype(BF16).astype(F32) * gtn.astype(F32), axis=0, keepdims=True)
        dgn_ref[cols, :] = gtn.astype(F32).T.astype(BF16)
        dp_ref[hp] = dot(kv_ref[1, g, win, :], gtn, ((1,), (0,)))
        for kb in range(8):
            rows = slice(kb * BLK, (kb + 1) * BLK)
            ds_ref[rows, cols] = (e_ref[rows, cols].astype(F32) * (dp_ref[hp, rows, :] - rd)).astype(BF16)
        qt = dot(kvt_ref[0, g, :, win], ds_ref[:, cols], ((1,), (0,))) * (SCALE * keep)
        dq_st[g, blk, lo] = qt[:, :128].T.astype(BF16)
        dq_st[g, blk, hi] = qt[:, 128:].T.astype(BF16)

    def head_cols(g):
        return pl.ds(pl.multiple_of((2 * core + g) * 512, 512), 512)

    def dq_copy(g, qb):
        half = lax.rem(qb, 2)
        return remote(
            dq_st.at[g, pl.ds(pl.multiple_of(qb * BLK, BLK), BLK), :],
            gq_ref.at[0, pl.ds(pl.multiple_of(half * BLK, BLK), BLK), head_cols(g)],
            dq_snd.at[g * 4 + qb], dq_rcv.at[core * 4 + g * 2 + half], at(prv_p, 0, lax.div(qb, 2)),
        )

    def o_copy(g, qb, local):
        half = lax.rem(qb, 2)
        src = o_st.at[g, pl.ds(pl.multiple_of(qb * BLK, BLK), BLK), :]
        dst = out_ref.at[0, pl.ds(pl.multiple_of(half * BLK, BLK), BLK), head_cols(g)]
        if local:
            return pltpu.make_async_copy(src, dst, o_sem.at[g * 4 + qb])
        return remote(src, dst, o_sem.at[g * 4 + qb], o_rcv.at[g * 2 + half], partner)

    def c2_copy(g, i):
        return remote(c2_st.at[g, i], c2_rx.at[g, i], c2_snd.at[g, i], c2_rcv.at[g, i], at(p, -2, core))

    def kv_final(g, i, which, stage, landing, snd, rcv, hop):
        return remote(
            stage.at[g, i, pl.ds(which * 256, 256), :],
            landing.at[i, :, pl.ds(pl.multiple_of((2 * core + g) * BLK, BLK), BLK)],
            snd.at[g, i, which], rcv.at[2 * core + g, i], at(prv_p, hop, which),
        )

    def c1_copy(g, i, which):
        return kv_final(g, i, which, c1_st, nxt_rx, c1_snd, c1_rcv, -1)

    def own_copy(g, i, which):
        return kv_final(g, i, which, own_st, own_rx, own_snd, own_rcv, 0)

    factor = (SCALE, 1.0)

    def send_own(g):
        for i in range(2):
            c2_copy(g, i).wait_recv()
            own_st[g, i, 0:128, :] = (acc_ref[i, g, 896:1024, :] * (factor[i] * keep)).astype(BF16)
            rest = acc_ref[i, g, 1024:1408, :] * factor[i] + c2_rx[g, i].astype(F32)
            own_st[g, i, 128:512, :] = (rest * keep).astype(BF16)
            for which in range(2):
                own_copy(g, i, which).start()

    def step(it, carry):
        g = lax.div(it, 4)
        qb = lax.rem(it, 4)

        @pl.when(qb == 0)
        def _():
            take_group(g)

        own_doc = doc_ref[0, 4 * chip + qb]
        hide = []
        for kb in range(7):
            spot = 4 * chip + qb + kb - 7
            seen = (doc_ref[0, jnp.maximum(spot, 0)] == own_doc) & (spot >= 0)
            hide.append(jnp.where(seen, 0.0, HIDE).astype(F32))
        for hp in range(2):
            pair(g, qb, hp, hide)
        win = pl.ds(pl.multiple_of(qb * BLK, BLK), WIN)
        acc_ref[1, g, win, :] += dot(e_ref[...], dgn_ref[...], ((1,), (0,)))
        acc_ref[0, g, win, :] += dot(ds_ref[...], q2_ref[...], ((1,), (0,)))
        dq_copy(g, qb).start()

        @pl.when(lax.div(qb, 2) == core)
        def _():
            o_copy(g, qb, True).start()

        @pl.when(lax.div(qb, 2) != core)
        def _():
            o_copy(g, qb, False).start()

        @pl.when(qb == 2)
        def _():
            for i in range(2):
                c2_st[g, i] = (acc_ref[i, g, 0:384, :] * factor[i]).astype(BF16)
                c2_copy(g, i).start()

        @pl.when(qb == 3)
        def _():
            for i in range(2):
                c1_st[g, i] = (acc_ref[i, g, 384:896, :] * (factor[i] * keep)).astype(BF16)
                for which in range(2):
                    c1_copy(g, i, which).start()

        @pl.when(it == 5)
        def _():
            send_own(0)

        return carry

    lax.fori_loop(0, 8, step, 0)
    send_own(1)

    for g in range(2):
        for copy in kv_one(g):
            copy.wait_send()
        for late in range(2):
            @pl.when(core == late)
            def _():
                for copy in kv_two(g, late):
                    copy.wait_send()
        kv_own(g)[1].wait_send()
        kv_own(g)[3].wait_send()
        io_copies(g)[1].wait_send()
        io_copies(g)[3].wait_send()
        for qb in range(4):
            dq_copy(g, qb).wait_send()
            @pl.when(qb // 2 == core)
            def _():
                o_copy(g, qb, True).wait()

            @pl.when(qb // 2 != core)
            def _():
                o_copy(g, qb, False).wait_send()
        for half in range(2):
            o_copy(g, half, False).wait_recv()
        for i in range(2):
            c2_copy(g, i).wait_send()
            for which in range(2):
                c1_copy(g, i, which).wait_send()
                own_copy(g, i, which).wait_send()
    for source in range(8):
        pltpu.make_async_copy(
            dq_st.at[0, pl.ds(0, BLK), :], dq_st.at[0, pl.ds(0, BLK), :], dq_rcv.at[source]
        ).wait()
    for i in range(2):
        for source in range(4):
            piece = nxt_rx.at[i, :, pl.ds(source * BLK, BLK)]
            pltpu.make_async_copy(piece, piece, c1_rcv.at[source, i]).wait()
            piece = own_rx.at[i, :, pl.ds(source * BLK, BLK)]
            pltpu.make_async_copy(piece, piece, own_rcv.at[source, i]).wait()
    gk_ref[0] = (nxt_rx[0].astype(F32) + own_rx[0].astype(F32)).astype(BF16)
    gv_ref[0] = (nxt_rx[1].astype(F32) + own_rx[1].astype(F32)).astype(BF16)


def solution(mesh):
    sections, shards = mesh.shape["pipe"], mesh.shape["ctx"]

    def body(queries, key_rows, value_rows, out_grad, doc_blocks):
        dma = pltpu.SemaphoreType.DMA
        vmem = pltpu.VMEM
        hbm = pl.BlockSpec(memory_space=pl.ANY)
        return pl.pallas_call(
            functools.partial(kernel, sections, shards),
            out_shape=(
                jax.ShapeDtypeStruct((1, 256, 2048), BF16),
                jax.ShapeDtypeStruct((1, 256, 2048), BF16),
                jax.ShapeDtypeStruct((1, 256, 512), BF16),
                jax.ShapeDtypeStruct((1, 256, 512), BF16),
            ),
            in_specs=[pl.BlockSpec(memory_space=pltpu.SMEM), hbm, hbm, hbm, hbm],
            out_specs=(
                hbm, hbm,
                pl.BlockSpec(memory_space=vmem), pl.BlockSpec(memory_space=vmem),
            ),
            scratch_shapes=[
                vmem((2, 512, 512), BF16), vmem((2, 512, 512), BF16),
                vmem((2, 2, ROWS, BLK), BF16), vmem((2, 2, BLK, ROWS), BF16),
                vmem((2, WIN, 256), F32), vmem((2, WIN, 256), F32),
                vmem((WIN, 512), BF16), vmem((WIN, 512), BF16),
                vmem((2, 2, ROWS, BLK), F32),
                vmem((512, BLK), BF16), vmem((512, BLK), BF16),
                vmem((2, 512, 512), BF16), vmem((2, 512, 512), BF16),
                vmem((2, 2, 384, BLK), BF16), vmem((2, 2, 512, BLK), BF16), vmem((2, 2, 512, BLK), BF16),
                vmem((2, 2, 384, BLK), BF16), vmem((2, 256, 512), BF16), vmem((2, 256, 512), BF16),
                dma((2, 2)), dma((2, 2)), dma((2, 2)),
                dma((2, 2)), dma((5, 2, 2)), dma((5, 2, 2)),
                dma((8,)), dma((4,)), dma((8,)), dma((8,)),
                dma((2, 2)), dma((2, 2)), dma((2, 2, 2)), dma((4, 2)), dma((2, 2, 2)), dma((4, 2)),
            ],
            compiler_params=pltpu.CompilerParams(
                collective_id=0, has_side_effects=True, vmem_limit_bytes=48 * 1024 * 1024
            ),
        )(doc_blocks, queries, key_rows, value_rows, out_grad)

    tokens = P("pipe", "ctx", None)
    return jax.shard_map(
        body,
        mesh=mesh,
        in_specs=(tokens, tokens, tokens, tokens, P("pipe", None)),
        out_specs=(tokens, tokens, tokens, tokens),
        check_vma=False,
    )
```

```python
import functools
import math

import jax
import jax.numpy as jnp
from jax import lax
from jax.experimental import pallas as pl
from jax.experimental.pallas import tpu as pltpu
from jax.sharding import PartitionSpec as P

MESH = pl.DeviceIdType.MESH
BF16 = jnp.bfloat16
F32 = jnp.float32
BLK = 128
SCALE = 1.0 / math.sqrt(128.0)
SCALE2 = SCALE * math.log2(math.e)
HIDE = 1e30
ROWS = 11 * BLK
WIN = 8 * BLK


def dot(a, b, dims):
    return lax.dot_general(a, b, (dims, ((), ())), preferred_element_type=F32)


def kernel(
    sections, shards,
    doc_hbm, q_hbm, k_hbm, v_hbm, g_hbm,
    out_ref, gq_ref, nxt_rx, own_rx,
    doc_ref, qb_ref, gb_ref, kv_ref, kvt_ref, s_ref, dp_ref, e_ref, ds_ref, acc_ref, dgn_ref, q2_ref,
    o_st, dq_st, c2_st, c1_st, own_st, c2_rx, rel_rx,
    doc_sem, io_loc, io_snd, io_rcv, kv_loc, kv_snd, kv_rcv, o_sem, o_rcv, dq_snd, dq_rcv,
    c2_snd, c2_rcv, rel_snd, rel_rcv, c1_snd, c1_rcv, own_snd, own_rcv,
):
    p = lax.axis_index("pipe")
    dev = lax.axis_index("ctx")
    core = lax.rem(dev, 2)
    chip = lax.div(dev, 2)
    chips = shards // 2
    pair_p = p + 1 - 2 * lax.rem(p, 2)
    even = lax.rem(p, 2) == 0
    has_prev, has_prev2 = chip >= 1, chip >= 2
    has_next, has_next2 = chip <= chips - 2, chip <= chips - 3
    sends_pipe, gets_pipe = p >= 1, p <= sections - 2
    sends_relay = even & (p >= 2) & has_prev
    gets_relay = even & (p <= sections - 3) & has_prev
    sends_last = ((p <= sections - 3) | (lax.rem(p, 2) == 1)) & has_prev
    gets_last = gets_pipe & has_next

    def at(section, hop, which):
        return (section, 2 * (chip + hop) + which)

    doc_copy = pltpu.make_async_copy(doc_hbm, doc_ref, doc_sem)
    doc_copy.start()
    partner = (p, 2 * chip + 1 - core)
    barrier = pltpu.get_barrier_semaphore()

    def greet(when, targets):
        @pl.when(when)
        def _():
            for target in targets():
                pl.semaphore_signal(barrier, inc=1, device_id=target, device_id_type=MESH)

    pl.semaphore_signal(barrier, inc=1, device_id=partner, device_id_type=MESH)
    greet(has_prev, lambda: [at(p, -1, which) for which in range(2)])
    greet(has_prev2, lambda: [at(p, -2, which) for which in range(2)])
    greet(has_next2, lambda: [at(p, 2, core)])
    greet(gets_pipe, lambda: [at(p + 1, 0, which) for which in range(2)])
    greet(gets_relay, lambda: [at(p + 2, 0, core)])
    greet(gets_last, lambda: [at(pair_p, 1, which) for which in range(2)])

    @pl.when(chip < 2)
    def _():
        kv_ref[:, :, 0:384, :] = jnp.zeros((2, 2, 384, BLK), BF16)

    @pl.when(chip < 1)
    def _():
        kv_ref[:, :, 384:896, :] = jnp.zeros((2, 2, 512, BLK), BF16)

    awaited = 1
    for when, count in ((has_next, 2), (has_next2, 2), (has_prev2, 1), (sends_pipe, 2), (sends_relay, 1), (sends_last, 2)):
        awaited = awaited + jnp.where(when, count, 0)
    pl.semaphore_wait(barrier, awaited)

    def remote(src, dst, snd, rcv, target):
        return pltpu.make_async_remote_copy(
            src_ref=src, dst_ref=dst, send_sem=snd, recv_sem=rcv,
            device_id=target, device_id_type=MESH,
        )

    def kv_cols(ref, rows, which, g):
        return ref.at[0, rows, pl.ds(pl.multiple_of((2 * which + g) * BLK, BLK), BLK)]

    kv_hbm = (k_hbm, v_hbm)
    io_hbm = (q_hbm, g_hbm)
    io_buf = (qb_ref, gb_ref)
    mine = pl.ds(pl.multiple_of(core * 256, 256), 256)
    whole = pl.ds(0, 256)

    def io_copies(g):
        copies = []
        for i in range(2):
            src = lambda which: io_hbm[i].at[0, :, pl.ds(pl.multiple_of(which * 1024 + g * 512, 512), 512)]
            dst = io_buf[i].at[g, mine, :]
            copies.append(pltpu.make_async_copy(src(core), dst, io_loc.at[g, i]))
            copies.append(remote(src(1 - core), dst, io_snd.at[g, i], io_rcv.at[g, i], partner))
        return copies

    def kv_own(g):
        copies = []
        for i in range(2):
            dst = kv_ref.at[i, g, pl.ds(pl.multiple_of(896 + core * 256, 128), 256), :]
            copies.append(pltpu.make_async_copy(kv_cols(kv_hbm[i], whole, core, g), dst, kv_loc.at[g, i]))
            copies.append(
                remote(kv_cols(kv_hbm[i], whole, 1 - core, g), dst, kv_snd.at[0, g, i], kv_rcv.at[0, g, i], partner)
            )
        return copies

    def kv_one(g):
        copies = []
        for which in range(2):
            for i in range(2):
                dst = kv_ref.at[i, g, pl.ds(pl.multiple_of(384 + core * 256, 128), 256), :]
                copies.append(
                    remote(
                        kv_cols(kv_hbm[i], whole, which, g), dst,
                        kv_snd.at[1 + which, g, i], kv_rcv.at[1 + core, g, i], at(p, 1, which),
                    )
                )
        return copies

    def kv_two(g, late):
        copies = []
        for which in range(2):
            for i in range(2):
                rows = pl.ds(128, 128) if late == 0 else whole
                to = pl.ds(0, 128) if late == 0 else pl.ds(128, 256)
                copies.append(
                    remote(
                        kv_cols(kv_hbm[i], rows, which, g), kv_ref.at[i, g, to, :],
                        kv_snd.at[3 + which, g, i], kv_rcv.at[3 + late, g, i], at(p, 2, which),
                    )
                )
        return copies

    for g in range(2):
        @pl.when(has_next)
        def _():
            for copy in kv_one(g):
                copy.start()

        for copy in kv_own(g) + io_copies(g):
            copy.start()

    acc_ref[...] = jnp.zeros_like(acc_ref)

    @pl.when(jnp.logical_not(has_next2))
    def _():
        c2_rx[...] = jnp.zeros_like(c2_rx)

    causal = lax.broadcasted_iota(jnp.int32, (BLK, 256), 0) <= lax.rem(
        lax.broadcasted_iota(jnp.int32, (BLK, 256), 1), BLK
    )

    def landed(ref, sem):
        pltpu.make_async_copy(ref, ref, sem).wait()

    def take_near(g):
        for i in range(2):
            landed(io_buf[i].at[g, whole, :], io_loc.at[g, i])
            landed(io_buf[i].at[g, whole, :], io_rcv.at[g, i])
            landed(kv_ref.at[i, g, whole, :], kv_loc.at[g, i])
            landed(kv_ref.at[i, g, whole, :], kv_rcv.at[0, g, i])

            @pl.when(has_prev)
            def _():
                landed(kv_ref.at[i, g, whole, :], kv_rcv.at[1, g, i])
                landed(kv_ref.at[i, g, whole, :], kv_rcv.at[2, g, i])
        for i in range(2):
            kvt_ref[i, g, :, 384:1408] = kv_ref[i, g, 384:1408, :].T

    def take_far(g):
        @pl.when(has_prev2)
        def _():
            for i in range(2):
                landed(kv_ref.at[i, g, pl.ds(0, 128), :], kv_rcv.at[3, g, i])
                landed(kv_ref.at[i, g, whole, :], kv_rcv.at[4, g, i])
        for i in range(2):
            kvt_ref[i, g, :, 0:384] = kv_ref[i, g, 0:384, :].T

    def lanes(hp):
        return slice(hp * 256, hp * 256 + 128), slice(hp * 256 + 128, hp * 256 + 256)

    def block(g, qb, hide):
        row = pl.multiple_of(qb * BLK, BLK)
        win = pl.ds(row, WIN)
        blk = pl.ds(row, BLK)
        tiles = [slice(kb * BLK, (kb + 1) * BLK) for kb in range(8)]
        top, total, inv, ot, gtn, rd = ([None, None] for _ in range(6))

        def cols(hp):
            return pl.ds(hp * 256, 256)

        def stack(ref, hp):
            lo, hi = lanes(hp)
            return jnp.concatenate([ref[g, blk, lo], ref[g, blk, hi]], 0)

        def scores(hp, part):
            if part == 0:
                q2_ref[cols(hp), :] = stack(qb_ref, hp)
            here = pl.ds(pl.multiple_of(row + part * 512, BLK), 512)
            s_ref[hp, part * 512:part * 512 + 512, :] = dot(kv_ref[0, g, here, :], q2_ref[cols(hp), :], ((1,), (1,)))

        def highs(hp, kbs):
            for kb in kbs:
                tile = s_ref[hp, tiles[kb], :]
                if kb == 7:
                    tile = jnp.where(causal, tile, -HIDE)
                    s_ref[hp, tiles[kb], :] = tile
                high = jnp.max(tile, axis=0, keepdims=True)
                if kb < 7:
                    high = high - hide[kb]
                top[hp] = high if top[hp] is None else jnp.maximum(top[hp], high)

        def exps(hp, kbs):
            for kb in kbs:
                off = top[hp] * SCALE2
                off = off + hide[kb] if kb < 7 else off
                e = jnp.exp2(s_ref[hp, tiles[kb], :] * SCALE2 - off)
                part = jnp.sum(e, axis=0, keepdims=True)
                total[hp] = part if total[hp] is None else total[hp] + part
                e_ref[tiles[kb], cols(hp)] = e.astype(BF16)

        def attend(hp):
            lo, hi = lanes(hp)
            inv[hp] = 1.0 / total[hp]
            gtn[hp] = (stack(gb_ref, hp).astype(F32).T * inv[hp]).astype(BF16)
            dgn_ref[cols(hp), :] = gtn[hp].astype(F32).T.astype(BF16)
            ot[hp] = dot(kvt_ref[1, g, :, win], e_ref[:, cols(hp)], ((1,), (0,))) * inv[hp]
            o_st[g, blk, lo] = ot[hp][:, :128].T.astype(BF16)
            o_st[g, blk, hi] = ot[hp][:, 128:].T.astype(BF16)
            rd[hp] = jnp.sum(ot[hp].astype(BF16).astype(F32) * gtn[hp].astype(F32), axis=0, keepdims=True)

        def prob_grads(hp):
            dp_ref[hp] = dot(kv_ref[1, g, win, :], gtn[hp], ((1,), (0,)))

        def score_grads(hp, kbs):
            for kb in kbs:
                ds_ref[tiles[kb], cols(hp)] = e_ref[tiles[kb], cols(hp)] * (dp_ref[hp, tiles[kb], :] - rd[hp]).astype(BF16)

        def query_grads(hp):
            lo, hi = lanes(hp)
            qt = dot(kvt_ref[0, g, :, win], ds_ref[:, cols(hp)], ((1,), (0,))) * SCALE
            dq_st[g, blk, lo] = qt[:, :128].T.astype(BF16)
            dq_st[g, blk, hi] = qt[:, 128:].T.astype(BF16)

        early, late = range(4), range(4, 8)
        scores(0, 0)
        scores(0, 1)
        highs(0, range(8))
        scores(1, 0)
        exps(0, early)
        scores(1, 1)
        exps(0, late)
        attend(0)
        highs(1, range(8))
        prob_grads(0)
        exps(1, range(8))
        score_grads(0, range(8))
        attend(1)
        prob_grads(1)
        query_grads(0)
        score_grads(1, range(8))
        acc_ref[1, g, win, :] += dot(e_ref[...], dgn_ref[...], ((1,), (0,)))
        query_grads(1)
        acc_ref[0, g, win, :] += dot(ds_ref[...], q2_ref[...], ((1,), (0,)))

    def head_cols(g):
        return pl.ds(pl.multiple_of((2 * core + g) * 512, 512), 512)

    def dq_copy(g, qb):
        half = lax.rem(qb, 2)
        return remote(
            dq_st.at[g, pl.ds(pl.multiple_of(qb * BLK, BLK), BLK), :],
            gq_ref.at[0, pl.ds(pl.multiple_of(half * BLK, BLK), BLK), head_cols(g)],
            dq_snd.at[g * 4 + qb], dq_rcv.at[core * 4 + g * 2 + half], at(p - 1, 0, lax.div(qb, 2)),
        )

    def o_copy(g, qb, local):
        half = lax.rem(qb, 2)
        src = o_st.at[g, pl.ds(pl.multiple_of(qb * BLK, BLK), BLK), :]
        dst = out_ref.at[0, pl.ds(pl.multiple_of(half * BLK, BLK), BLK), head_cols(g)]
        if local:
            return pltpu.make_async_copy(src, dst, o_sem.at[g * 4 + qb])
        return remote(src, dst, o_sem.at[g * 4 + qb], o_rcv.at[g * 2 + half], partner)

    def c2_copy(g, i):
        return remote(c2_st.at[g, i], c2_rx.at[g, i], c2_snd.at[g, i], c2_rcv.at[g, i], at(p, -2, core))

    def rel_copy(g, i):
        return remote(c1_st.at[g, i], rel_rx.at[g, i], rel_snd.at[g, i], rel_rcv.at[g, i], at(p - 2, 0, core))

    def kv_final(g, i, which, stage, landing, snd, rcv, target):
        return remote(
            stage.at[g, i, pl.ds(which * 256, 256), :],
            landing.at[i, :, pl.ds(pl.multiple_of((2 * core + g) * BLK, BLK), BLK)],
            snd.at[g, i, which], rcv.at[2 * core + g, i], target,
        )

    def last_copy(g, i, which, stage):
        return kv_final(g, i, which, stage, nxt_rx, c1_snd, c1_rcv, at(pair_p, -1, which))

    def own_copy(g, i, which):
        return kv_final(g, i, which, own_st, own_rx, own_snd, own_rcv, at(p - 1, 0, which))

    factor = (SCALE, 1.0)

    def send_own(g):
        @pl.when(has_next2)
        def _():
            for i in range(2):
                c2_copy(g, i).wait_recv()

        @pl.when(sends_pipe)
        def _():
            for i in range(2):
                own_st[g, i, 0:128, :] = (acc_ref[i, g, 896:1024, :] * factor[i]).astype(BF16)
                rest = acc_ref[i, g, 1024:1408, :] * factor[i] + c2_rx[g, i].astype(F32)
                own_st[g, i, 128:512, :] = rest.astype(BF16)
                for which in range(2):
                    own_copy(g, i, which).start()

    def forward(g):
        @pl.when(gets_relay)
        def _():
            for i in range(2):
                rel_copy(g, i).wait_recv()
                for which in range(2):
                    last_copy(g, i, which, rel_rx).start()

    def step(it, carry):
        g = jnp.where((it == 1) | (it >= 5), 1, 0)
        qb = jnp.where(it < 2, 3, jnp.where(it < 5, 4 - it, 7 - it))

        @pl.when(it < 2)
        def _():
            take_near(g)

        @pl.when(it == 0)
        def _():
            for late in range(2):
                @pl.when(has_next2 & (core == late))
                def _():
                    for group in range(2):
                        for copy in kv_two(group, late):
                            copy.start()

        @pl.when((it == 2) | (it == 5))
        def _():
            take_far(g)

        own_doc = doc_ref[0, 4 * chip + qb]
        hide = []
        for kb in range(7):
            spot = 4 * chip + qb + kb - 7
            seen = (doc_ref[0, jnp.maximum(spot, 0)] == own_doc) & (spot >= 0)
            hide.append(jnp.where(seen, 0.0, HIDE).astype(F32))
        block(g, qb, hide)

        @pl.when(sends_pipe)
        def _():
            dq_copy(g, qb).start()

        @pl.when(lax.div(qb, 2) == core)
        def _():
            o_copy(g, qb, True).start()

        @pl.when(lax.div(qb, 2) != core)
        def _():
            o_copy(g, qb, False).start()

        done = (it == 4) | (it == 7)

        @pl.when(done & has_prev2)
        def _():
            for i in range(2):
                c2_st[g, i] = (acc_ref[i, g, 0:384, :] * factor[i]).astype(BF16)
                c2_copy(g, i).start()

        @pl.when(done & has_prev & sends_pipe)
        def _():
            for i in range(2):
                c1_st[g, i] = (acc_ref[i, g, 384:896, :] * factor[i]).astype(BF16)

                @pl.when(even)
                def _():
                    rel_copy(g, i).start()

                @pl.when(jnp.logical_not(even))
                def _():
                    for which in range(2):
                        last_copy(g, i, which, c1_st).start()

        @pl.when(it == 6)
        def _():
            send_own(0)
            forward(0)

        return carry

    doc_copy.wait()
    lax.fori_loop(0, 8, step, 0)
    send_own(1)
    forward(1)

    for g in range(2):
        @pl.when(has_next)
        def _():
            for copy in kv_one(g):
                copy.wait_send()

        for late in range(2):
            @pl.when(has_next2 & (core == late))
            def _():
                for copy in kv_two(g, late):
                    copy.wait_send()
        for copy in kv_own(g)[1::2] + io_copies(g)[1::2]:
            copy.wait_send()
        for qb in range(4):
            @pl.when(qb // 2 == core)
            def _():
                o_copy(g, qb, True).wait()

            @pl.when(qb // 2 != core)
            def _():
                o_copy(g, qb, False).wait_send()
        for half in range(2):
            o_copy(g, half, False).wait_recv()

        @pl.when(has_prev2)
        def _():
            for i in range(2):
                c2_copy(g, i).wait_send()

        @pl.when(sends_relay)
        def _():
            for i in range(2):
                rel_copy(g, i).wait_send()

        @pl.when(sends_last)
        def _():
            for i in range(2):
                for which in range(2):
                    last_copy(g, i, which, rel_rx).wait_send()

        @pl.when(sends_pipe)
        def _():
            for qb in range(4):
                dq_copy(g, qb).wait_send()
            for i in range(2):
                for which in range(2):
                    own_copy(g, i, which).wait_send()

    @pl.when(gets_pipe)
    def _():
        for source in range(8):
            landed(dq_st.at[0, pl.ds(0, BLK), :], dq_rcv.at[source])
        for i in range(2):
            for source in range(4):
                landed(own_rx.at[i, :, pl.ds(source * BLK, BLK)], own_rcv.at[source, i])

    @pl.when(gets_last)
    def _():
        for i in range(2):
            for source in range(4):
                landed(nxt_rx.at[i, :, pl.ds(source * BLK, BLK)], c1_rcv.at[source, i])


def finish(sections, shards, out_ref, gq_ref, nxt_ref, own_ref, out_hbm, gq_hbm, gk_hbm, gv_hbm, sum_ref, zero_ref, sems):
    gets_pipe = lax.axis_index("pipe") <= sections - 2
    gets_last = gets_pipe & (lax.axis_index("ctx") < shards - 2)
    out_copy = pltpu.make_async_copy(out_ref, out_hbm, sems.at[0])
    out_copy.start()

    @pl.when(gets_pipe)
    def _():
        pltpu.make_async_copy(gq_ref, gq_hbm, sems.at[1]).start()

    @pl.when(jnp.logical_not(gets_pipe))
    def _():
        zero_ref[...] = jnp.zeros_like(zero_ref)
        pltpu.make_async_copy(zero_ref, gq_hbm, sems.at[1]).start()

    grads = (gk_hbm, gv_hbm)
    for i in range(2):
        last = jnp.where(gets_last, nxt_ref[i].astype(F32), 0.0)
        sum_ref[i] = jnp.where(gets_pipe, last + own_ref[i].astype(F32), 0.0).astype(BF16)
        pltpu.make_async_copy(sum_ref.at[pl.ds(i, 1)], grads[i], sems.at[2 + i]).start()
    out_copy.wait()
    pltpu.make_async_copy(zero_ref, gq_hbm, sems.at[1]).wait()
    for i in range(2):
        pltpu.make_async_copy(sum_ref.at[pl.ds(i, 1)], grads[i], sems.at[2 + i]).wait()


def solution(mesh):
    sections, shards = mesh.shape["pipe"], mesh.shape["ctx"]

    def body(queries, key_rows, value_rows, out_grad, doc_blocks):
        dma = pltpu.SemaphoreType.DMA
        vmem = pltpu.VMEM
        hbm = pl.BlockSpec(memory_space=pltpu.HBM)
        near = pl.BlockSpec(memory_space=vmem)
        any_place = pl.BlockSpec(memory_space=pl.ANY)
        wide = jax.ShapeDtypeStruct((1, 256, 2048), BF16)
        slim = jax.ShapeDtypeStruct((1, 256, 512), BF16)
        both = jax.ShapeDtypeStruct((2, 256, 512), BF16)
        pinned = [pltpu.with_memory_space_constraint(x, pltpu.HBM) for x in (doc_blocks, queries, key_rows, value_rows, out_grad)]
        parts = pl.pallas_call(
            functools.partial(kernel, sections, shards),
            out_shape=(wide, wide, both, both),
            in_specs=[hbm] * 5,
            out_specs=(any_place,) * 4,
            scratch_shapes=[
                pltpu.SMEM((1, 64), jnp.int32),
                vmem((2, 512, 512), BF16), vmem((2, 512, 512), BF16),
                vmem((2, 2, ROWS, BLK), BF16), vmem((2, 2, BLK, ROWS), BF16),
                vmem((2, WIN, 256), F32), vmem((2, WIN, 256), F32),
                vmem((WIN, 512), BF16), vmem((WIN, 512), BF16),
                vmem((2, 2, ROWS, BLK), F32),
                vmem((512, BLK), BF16), vmem((512, BLK), BF16),
                vmem((2, 512, 512), BF16), vmem((2, 512, 512), BF16),
                vmem((2, 2, 384, BLK), BF16), vmem((2, 2, 512, BLK), BF16), vmem((2, 2, 512, BLK), BF16),
                vmem((2, 2, 384, BLK), BF16), vmem((2, 2, 512, BLK), BF16),
                dma, dma((2, 2)), dma((2, 2)), dma((2, 2)),
                dma((2, 2)), dma((5, 2, 2)), dma((5, 2, 2)),
                dma((8,)), dma((4,)), dma((8,)), dma((8,)),
                dma((2, 2)), dma((2, 2)), dma((2, 2)), dma((2, 2)),
                dma((2, 2, 2)), dma((4, 2)), dma((2, 2, 2)), dma((4, 2)),
            ],
            compiler_params=pltpu.CompilerParams(
                collective_id=0, has_side_effects=True, vmem_limit_bytes=48 * 1048576
            ),
        )(*pinned)
        return pl.pallas_call(
            functools.partial(finish, sections, shards),
            out_shape=(wide, wide, slim, slim),
            in_specs=[any_place, any_place, near, near],
            out_specs=(hbm,) * 4,
            scratch_shapes=[vmem((2, 256, 512), BF16), vmem((1, 256, 2048), BF16), dma((4,))],
            compiler_params=pltpu.CompilerParams(vmem_limit_bytes=8 * 1048576),
        )(*parts)

    tokens = P("pipe", "ctx", None)
    return jax.shard_map(
        body,
        mesh=mesh,
        in_specs=(tokens, tokens, tokens, tokens, P("pipe", None)),
        out_specs=(tokens, tokens, tokens, tokens),
        check_vma=False,
    )
```

```python
import functools
import math

import jax
import jax.numpy as jnp
from jax import lax
from jax.experimental import pallas as pl
from jax.experimental.pallas import tpu as pltpu
from jax.sharding import PartitionSpec as P

MESH = pl.DeviceIdType.MESH
BF16 = jnp.bfloat16
F32 = jnp.float32
BLK = 128
SCALE = 1.0 / math.sqrt(128.0)
SCALE2 = SCALE * math.log2(math.e)
HIDE = 1e30
ROWS = 11 * BLK
WIN = 8 * BLK


def dot(a, b, dims):
    return lax.dot_general(a, b, (dims, ((), ())), preferred_element_type=F32)


def kernel(
    sections, shards,
    doc_hbm, q_hbm, k_hbm, v_hbm, g_hbm,
    out_ref, gq_ref, nxt_rx, own_rx,
    doc_ref, qb_ref, gb_ref, kv_ref, kvt_ref, s_ref, dp_ref, e_ref, ds_ref, acc_ref, dgn_ref, q2_ref,
    o_st, dq_st, c2_st, c1_st, own_st, c2_rx, rel_rx,
    doc_sem, io_loc, io_snd, io_rcv, kv_loc, kv_snd, kv_rcv, o_sem, o_rcv, dq_snd, dq_rcv,
    c2_snd, c2_rcv, rel_snd, rel_rcv, c1_snd, c1_rcv, own_snd, own_rcv,
):
    p = lax.axis_index("pipe")
    dev = lax.axis_index("ctx")
    core = lax.rem(dev, 2)
    chip = lax.div(dev, 2)
    chips = shards // 2
    pair_p = p + 1 - 2 * lax.rem(p, 2)
    even = lax.rem(p, 2) == 0
    has_prev, has_prev2 = chip >= 1, chip >= 2
    has_next, has_next2 = chip <= chips - 2, chip <= chips - 3
    sends_pipe, gets_pipe = p >= 1, p <= sections - 2
    sends_relay = even & (p >= 2) & has_prev
    gets_relay = even & (p <= sections - 3) & has_prev
    sends_last = ((p <= sections - 3) | (lax.rem(p, 2) == 1)) & has_prev
    gets_last = gets_pipe & has_next

    def at(section, hop, which):
        return (section, 2 * (chip + hop) + which)

    doc_copy = pltpu.make_async_copy(doc_hbm, doc_ref, doc_sem)
    doc_copy.start()
    partner = (p, 2 * chip + 1 - core)
    barrier = pltpu.get_barrier_semaphore()

    def greet(when, targets):
        @pl.when(when)
        def _():
            for target in targets():
                pl.semaphore_signal(barrier, inc=1, device_id=target, device_id_type=MESH)

    pl.semaphore_signal(barrier, inc=1, device_id=partner, device_id_type=MESH)
    greet(has_prev, lambda: [at(p, -1, which) for which in range(2)])
    greet(has_prev2, lambda: [at(p, -2, which) for which in range(2)])
    greet(has_next2, lambda: [at(p, 2, core)])
    greet(gets_pipe, lambda: [at(p + 1, 0, which) for which in range(2)])
    greet(gets_relay, lambda: [at(p + 2, 0, core)])
    greet(gets_last, lambda: [at(pair_p, 1, which) for which in range(2)])

    @pl.when(chip < 2)
    def _():
        kv_ref[:, :, 0:384, :] = jnp.zeros((2, 2, 384, BLK), BF16)

    @pl.when(chip < 1)
    def _():
        kv_ref[:, :, 384:896, :] = jnp.zeros((2, 2, 512, BLK), BF16)

    awaited = 1
    for when, count in ((has_next, 2), (has_next2, 2), (has_prev2, 1), (sends_pipe, 2), (sends_relay, 1), (sends_last, 2)):
        awaited = awaited + jnp.where(when, count, 0)
    pl.semaphore_wait(barrier, awaited)

    def remote(src, dst, snd, rcv, target):
        return pltpu.make_async_remote_copy(
            src_ref=src, dst_ref=dst, send_sem=snd, recv_sem=rcv,
            device_id=target, device_id_type=MESH,
        )

    def kv_cols(ref, rows, which, g):
        return ref.at[0, rows, pl.ds(pl.multiple_of((2 * which + g) * BLK, BLK), BLK)]

    kv_hbm = (k_hbm, v_hbm)
    io_hbm = (q_hbm, g_hbm)
    io_buf = (qb_ref, gb_ref)
    mine = pl.ds(pl.multiple_of(core * 256, 256), 256)
    whole = pl.ds(0, 256)

    def io_copies(g):
        copies = []
        for i in range(2):
            src = lambda which: io_hbm[i].at[0, :, pl.ds(pl.multiple_of(which * 1024 + g * 512, 512), 512)]
            dst = io_buf[i].at[g, mine, :]
            copies.append(pltpu.make_async_copy(src(core), dst, io_loc.at[g, i]))
            copies.append(remote(src(1 - core), dst, io_snd.at[g, i], io_rcv.at[g, i], partner))
        return copies

    def kv_own(g):
        copies = []
        for i in range(2):
            dst = kv_ref.at[i, g, pl.ds(pl.multiple_of(896 + core * 256, 128), 256), :]
            copies.append(pltpu.make_async_copy(kv_cols(kv_hbm[i], whole, core, g), dst, kv_loc.at[g, i]))
            copies.append(
                remote(kv_cols(kv_hbm[i], whole, 1 - core, g), dst, kv_snd.at[0, g, i], kv_rcv.at[0, g, i], partner)
            )
        return copies

    def kv_one(g):
        copies = []
        for which in range(2):
            for i in range(2):
                dst = kv_ref.at[i, g, pl.ds(pl.multiple_of(384 + core * 256, 128), 256), :]
                copies.append(
                    remote(
                        kv_cols(kv_hbm[i], whole, which, g), dst,
                        kv_snd.at[1 + which, g, i], kv_rcv.at[1 + core, g, i], at(p, 1, which),
                    )
                )
        return copies

    def kv_two(g, late):
        copies = []
        for which in range(2):
            for i in range(2):
                rows = pl.ds(128, 128) if late == 0 else whole
                to = pl.ds(0, 128) if late == 0 else pl.ds(128, 256)
                copies.append(
                    remote(
                        kv_cols(kv_hbm[i], rows, which, g), kv_ref.at[i, g, to, :],
                        kv_snd.at[3 + which, g, i], kv_rcv.at[3 + late, g, i], at(p, 2, which),
                    )
                )
        return copies

    for g in range(2):
        @pl.when(has_next)
        def _():
            for copy in kv_one(g):
                copy.start()

        for copy in kv_own(g) + io_copies(g):
            copy.start()

    acc_ref[...] = jnp.zeros_like(acc_ref)

    @pl.when(jnp.logical_not(has_next2))
    def _():
        c2_rx[...] = jnp.zeros_like(c2_rx)

    causal = lax.broadcasted_iota(jnp.int32, (BLK, 256), 0) <= lax.rem(
        lax.broadcasted_iota(jnp.int32, (BLK, 256), 1), BLK
    )

    def landed(ref, sem):
        pltpu.make_async_copy(ref, ref, sem).wait()

    def take_near(g):
        for i in range(2):
            landed(io_buf[i].at[g, whole, :], io_loc.at[g, i])
            landed(io_buf[i].at[g, whole, :], io_rcv.at[g, i])
            landed(kv_ref.at[i, g, whole, :], kv_loc.at[g, i])
            landed(kv_ref.at[i, g, whole, :], kv_rcv.at[0, g, i])

            @pl.when(has_prev)
            def _():
                landed(kv_ref.at[i, g, whole, :], kv_rcv.at[1, g, i])
                landed(kv_ref.at[i, g, whole, :], kv_rcv.at[2, g, i])
        for i in range(2):
            kvt_ref[i, g, :, 384:1408] = kv_ref[i, g, 384:1408, :].T

    def take_far(g):
        @pl.when(has_prev2)
        def _():
            for i in range(2):
                landed(kv_ref.at[i, g, pl.ds(0, 128), :], kv_rcv.at[3, g, i])
                landed(kv_ref.at[i, g, whole, :], kv_rcv.at[4, g, i])
        for i in range(2):
            kvt_ref[i, g, :, 0:384] = kv_ref[i, g, 0:384, :].T

    def lanes(hp):
        return slice(hp * 256, hp * 256 + 128), slice(hp * 256 + 128, hp * 256 + 256)

    def block(g, qb, hide):
        row = pl.multiple_of(qb * BLK, BLK)
        win = pl.ds(row, WIN)
        blk = pl.ds(row, BLK)
        tiles = [slice(kb * BLK, (kb + 1) * BLK) for kb in range(8)]
        top, total, inv, ot, gtn, rd = ([None, None] for _ in range(6))

        def cols(hp):
            return pl.ds(hp * 256, 256)

        def stack(ref, hp):
            lo, hi = lanes(hp)
            return jnp.concatenate([ref[g, blk, lo], ref[g, blk, hi]], 0)

        def scores(hp, part):
            if part == 0:
                q2_ref[cols(hp), :] = stack(qb_ref, hp)
            here = pl.ds(pl.multiple_of(row + part * 512, BLK), 512)
            s_ref[hp, part * 512:part * 512 + 512, :] = dot(kv_ref[0, g, here, :], q2_ref[cols(hp), :], ((1,), (1,)))

        def highs(hp, kbs):
            for kb in kbs:
                tile = s_ref[hp, tiles[kb], :]
                if kb == 7:
                    tile = jnp.where(causal, tile, -HIDE)
                    s_ref[hp, tiles[kb], :] = tile
                high = jnp.max(tile, axis=0, keepdims=True)
                if kb < 7:
                    high = high - hide[kb]
                top[hp] = high if top[hp] is None else jnp.maximum(top[hp], high)

        def exps(hp, kbs):
            for kb in kbs:
                off = top[hp] * SCALE2
                off = off + hide[kb] if kb < 7 else off
                e = jnp.exp2(s_ref[hp, tiles[kb], :] * SCALE2 - off)
                part = jnp.sum(e, axis=0, keepdims=True)
                total[hp] = part if total[hp] is None else total[hp] + part
                e_ref[tiles[kb], cols(hp)] = e.astype(BF16)

        def attend(hp):
            lo, hi = lanes(hp)
            inv[hp] = 1.0 / total[hp]
            gtn[hp] = (stack(gb_ref, hp).astype(F32).T * inv[hp]).astype(BF16)
            dgn_ref[cols(hp), :] = gtn[hp].astype(F32).T.astype(BF16)
            ot[hp] = dot(kvt_ref[1, g, :, win], e_ref[:, cols(hp)], ((1,), (0,))) * inv[hp]
            o_st[g, blk, lo] = ot[hp][:, :128].T.astype(BF16)
            o_st[g, blk, hi] = ot[hp][:, 128:].T.astype(BF16)
            rd[hp] = jnp.sum(ot[hp].astype(BF16).astype(F32) * gtn[hp].astype(F32), axis=0, keepdims=True)

        def prob_grads(hp):
            dp_ref[hp] = dot(kv_ref[1, g, win, :], gtn[hp], ((1,), (0,)))

        def score_grads(hp, kbs):
            for kb in kbs:
                ds_ref[tiles[kb], cols(hp)] = e_ref[tiles[kb], cols(hp)] * (dp_ref[hp, tiles[kb], :] - rd[hp]).astype(BF16)

        def query_grads(hp):
            lo, hi = lanes(hp)
            qt = dot(kvt_ref[0, g, :, win], ds_ref[:, cols(hp)], ((1,), (0,))) * SCALE
            dq_st[g, blk, lo] = qt[:, :128].T.astype(BF16)
            dq_st[g, blk, hi] = qt[:, 128:].T.astype(BF16)

        early, late = range(4), range(4, 8)
        scores(0, 0)
        scores(0, 1)
        highs(0, range(8))
        scores(1, 0)
        exps(0, early)
        scores(1, 1)
        exps(0, late)
        attend(0)
        highs(1, range(8))
        prob_grads(0)
        exps(1, range(8))
        score_grads(0, range(8))
        attend(1)
        prob_grads(1)
        query_grads(0)
        score_grads(1, range(8))
        query_grads(1)

        @pl.when(sends_pipe)
        def _():
            dq_copy(g, qb).start()

        acc_ref[1, g, win, :] += dot(e_ref[...], dgn_ref[...], ((1,), (0,)))
        acc_ref[0, g, win, :] += dot(ds_ref[...], q2_ref[...], ((1,), (0,)))

    def head_cols(g):
        return pl.ds(pl.multiple_of((2 * core + g) * 512, 512), 512)

    def dq_copy(g, qb):
        half = lax.rem(qb, 2)
        return remote(
            dq_st.at[g, pl.ds(pl.multiple_of(qb * BLK, BLK), BLK), :],
            gq_ref.at[0, pl.ds(pl.multiple_of(half * BLK, BLK), BLK), head_cols(g)],
            dq_snd.at[g * 4 + qb], dq_rcv.at[core * 4 + g * 2 + half], at(p - 1, 0, lax.div(qb, 2)),
        )

    def o_copy(g, qb, local):
        half = lax.rem(qb, 2)
        src = o_st.at[g, pl.ds(pl.multiple_of(qb * BLK, BLK), BLK), :]
        dst = out_ref.at[0, pl.ds(pl.multiple_of(half * BLK, BLK), BLK), head_cols(g)]
        if local:
            return pltpu.make_async_copy(src, dst, o_sem.at[g * 4 + qb])
        return remote(src, dst, o_sem.at[g * 4 + qb], o_rcv.at[g * 2 + half], partner)

    def c2_copy(g, i):
        return remote(c2_st.at[g, i], c2_rx.at[g, i], c2_snd.at[g, i], c2_rcv.at[g, i], at(p, -2, core))

    def rel_copy(g, i):
        return remote(c1_st.at[g, i], rel_rx.at[g, i], rel_snd.at[g, i], rel_rcv.at[g, i], at(p - 2, 0, core))

    def kv_final(g, i, which, stage, landing, snd, rcv, target):
        return remote(
            stage.at[g, i, pl.ds(which * 256, 256), :],
            landing.at[i, :, pl.ds(pl.multiple_of((2 * core + g) * BLK, BLK), BLK)],
            snd.at[g, i, which], rcv.at[2 * core + g, i], target,
        )

    def last_copy(g, i, which, stage):
        return kv_final(g, i, which, stage, nxt_rx, c1_snd, c1_rcv, at(pair_p, -1, which))

    def own_copy(g, i, which):
        return kv_final(g, i, which, own_st, own_rx, own_snd, own_rcv, at(p - 1, 0, which))

    factor = (SCALE, 1.0)

    def send_own(g):
        @pl.when(has_next2)
        def _():
            for i in range(2):
                c2_copy(g, i).wait_recv()

        @pl.when(sends_pipe)
        def _():
            for i in range(2):
                own_st[g, i, 0:128, :] = (acc_ref[i, g, 896:1024, :] * factor[i]).astype(BF16)
                rest = acc_ref[i, g, 1024:1408, :] * factor[i] + c2_rx[g, i].astype(F32)
                own_st[g, i, 128:512, :] = rest.astype(BF16)
                for which in range(2):
                    own_copy(g, i, which).start()

    def forward(g):
        @pl.when(gets_relay)
        def _():
            for i in range(2):
                rel_copy(g, i).wait_recv()
                for which in range(2):
                    last_copy(g, i, which, rel_rx).start()

    def step(it, carry):
        g = jnp.where((it == 1) | (it >= 5), 1, 0)
        qb = jnp.where(it < 2, 3, jnp.where(it < 5, 4 - it, 7 - it))

        @pl.when(it < 2)
        def _():
            take_near(g)

        @pl.when(it == 0)
        def _():
            for late in range(2):
                @pl.when(has_next2 & (core == late))
                def _():
                    for group in range(2):
                        for copy in kv_two(group, late):
                            copy.start()

        @pl.when((it == 2) | (it == 5))
        def _():
            take_far(g)

        own_doc = doc_ref[0, 4 * chip + qb]
        hide = []
        for kb in range(7):
            spot = 4 * chip + qb + kb - 7
            seen = (doc_ref[0, jnp.maximum(spot, 0)] == own_doc) & (spot >= 0)
            hide.append(jnp.where(seen, 0.0, HIDE).astype(F32))
        block(g, qb, hide)

        @pl.when(lax.div(qb, 2) == core)
        def _():
            o_copy(g, qb, True).start()

        @pl.when(lax.div(qb, 2) != core)
        def _():
            o_copy(g, qb, False).start()

        done = (it == 4) | (it == 7)

        @pl.when(done & has_prev2)
        def _():
            for i in range(2):
                c2_st[g, i] = (acc_ref[i, g, 0:384, :] * factor[i]).astype(BF16)
                c2_copy(g, i).start()

        @pl.when(done & has_prev & sends_pipe)
        def _():
            for i in range(2):
                c1_st[g, i] = (acc_ref[i, g, 384:896, :] * factor[i]).astype(BF16)

                @pl.when(even)
                def _():
                    rel_copy(g, i).start()

                @pl.when(jnp.logical_not(even))
                def _():
                    for which in range(2):
                        last_copy(g, i, which, c1_st).start()

        @pl.when(it == 6)
        def _():
            send_own(0)
            forward(0)

        return carry

    doc_copy.wait()
    lax.fori_loop(0, 8, step, 0)
    send_own(1)
    forward(1)

    for g in range(2):
        @pl.when(has_next)
        def _():
            for copy in kv_one(g):
                copy.wait_send()

        for late in range(2):
            @pl.when(has_next2 & (core == late))
            def _():
                for copy in kv_two(g, late):
                    copy.wait_send()
        for copy in kv_own(g)[1::2] + io_copies(g)[1::2]:
            copy.wait_send()
        for qb in range(4):
            @pl.when(qb // 2 == core)
            def _():
                o_copy(g, qb, True).wait()

            @pl.when(qb // 2 != core)
            def _():
                o_copy(g, qb, False).wait_send()
        for half in range(2):
            o_copy(g, half, False).wait_recv()

        @pl.when(has_prev2)
        def _():
            for i in range(2):
                c2_copy(g, i).wait_send()

        @pl.when(sends_relay)
        def _():
            for i in range(2):
                rel_copy(g, i).wait_send()

        @pl.when(sends_last)
        def _():
            for i in range(2):
                for which in range(2):
                    last_copy(g, i, which, rel_rx).wait_send()

        @pl.when(sends_pipe)
        def _():
            for qb in range(4):
                dq_copy(g, qb).wait_send()
            for i in range(2):
                for which in range(2):
                    own_copy(g, i, which).wait_send()

    @pl.when(gets_pipe)
    def _():
        for source in range(8):
            landed(dq_st.at[0, pl.ds(0, BLK), :], dq_rcv.at[source])
        for i in range(2):
            for source in range(4):
                landed(own_rx.at[i, :, pl.ds(source * BLK, BLK)], own_rcv.at[source, i])

    @pl.when(gets_last)
    def _():
        for i in range(2):
            for source in range(4):
                landed(nxt_rx.at[i, :, pl.ds(source * BLK, BLK)], c1_rcv.at[source, i])


def finish(sections, shards, out_ref, gq_ref, nxt_ref, own_ref, out_hbm, gq_hbm, gk_hbm, gv_hbm, sum_ref, zero_ref, sems):
    gets_pipe = lax.axis_index("pipe") <= sections - 2
    gets_last = gets_pipe & (lax.axis_index("ctx") < shards - 2)
    out_copy = pltpu.make_async_copy(out_ref, out_hbm, sems.at[0])
    out_copy.start()

    @pl.when(gets_pipe)
    def _():
        pltpu.make_async_copy(gq_ref, gq_hbm, sems.at[1]).start()

    @pl.when(jnp.logical_not(gets_pipe))
    def _():
        zero_ref[...] = jnp.zeros_like(zero_ref)
        pltpu.make_async_copy(zero_ref, gq_hbm, sems.at[1]).start()

    grads = (gk_hbm, gv_hbm)
    for i in range(2):
        last = jnp.where(gets_last, nxt_ref[i].astype(F32), 0.0)
        sum_ref[i] = jnp.where(gets_pipe, last + own_ref[i].astype(F32), 0.0).astype(BF16)
        pltpu.make_async_copy(sum_ref.at[pl.ds(i, 1)], grads[i], sems.at[2 + i]).start()
    out_copy.wait()
    pltpu.make_async_copy(zero_ref, gq_hbm, sems.at[1]).wait()
    for i in range(2):
        pltpu.make_async_copy(sum_ref.at[pl.ds(i, 1)], grads[i], sems.at[2 + i]).wait()


def solution(mesh):
    sections, shards = mesh.shape["pipe"], mesh.shape["ctx"]

    def body(queries, key_rows, value_rows, out_grad, doc_blocks):
        dma = pltpu.SemaphoreType.DMA
        vmem = pltpu.VMEM
        hbm = pl.BlockSpec(memory_space=pltpu.HBM)
        near = pl.BlockSpec(memory_space=vmem)
        any_place = pl.BlockSpec(memory_space=pl.ANY)
        wide = jax.ShapeDtypeStruct((1, 256, 2048), BF16)
        slim = jax.ShapeDtypeStruct((1, 256, 512), BF16)
        both = jax.ShapeDtypeStruct((2, 256, 512), BF16)
        pinned = [pltpu.with_memory_space_constraint(x, pltpu.HBM) for x in (doc_blocks, queries, key_rows, value_rows, out_grad)]
        parts = pl.pallas_call(
            functools.partial(kernel, sections, shards),
            out_shape=(wide, wide, both, both),
            in_specs=[hbm] * 5,
            out_specs=(any_place,) * 4,
            scratch_shapes=[
                pltpu.SMEM((1, 64), jnp.int32),
                vmem((2, 512, 512), BF16), vmem((2, 512, 512), BF16),
                vmem((2, 2, ROWS, BLK), BF16), vmem((2, 2, BLK, ROWS), BF16),
                vmem((2, WIN, 256), F32), vmem((2, WIN, 256), F32),
                vmem((WIN, 512), BF16), vmem((WIN, 512), BF16),
                vmem((2, 2, ROWS, BLK), F32),
                vmem((512, BLK), BF16), vmem((512, BLK), BF16),
                vmem((2, 512, 512), BF16), vmem((2, 512, 512), BF16),
                vmem((2, 2, 384, BLK), BF16), vmem((2, 2, 512, BLK), BF16), vmem((2, 2, 512, BLK), BF16),
                vmem((2, 2, 384, BLK), BF16), vmem((2, 2, 512, BLK), BF16),
                dma, dma((2, 2)), dma((2, 2)), dma((2, 2)),
                dma((2, 2)), dma((5, 2, 2)), dma((5, 2, 2)),
                dma((8,)), dma((4,)), dma((8,)), dma((8,)),
                dma((2, 2)), dma((2, 2)), dma((2, 2)), dma((2, 2)),
                dma((2, 2, 2)), dma((4, 2)), dma((2, 2, 2)), dma((4, 2)),
            ],
            compiler_params=pltpu.CompilerParams(
                collective_id=0, has_side_effects=True, vmem_limit_bytes=48 * 1048576
            ),
        )(*pinned)
        return pl.pallas_call(
            functools.partial(finish, sections, shards),
            out_shape=(wide, wide, slim, slim),
            in_specs=[any_place, any_place, near, near],
            out_specs=(hbm,) * 4,
            scratch_shapes=[vmem((2, 256, 512), BF16), vmem((1, 256, 2048), BF16), dma((4,))],
            compiler_params=pltpu.CompilerParams(vmem_limit_bytes=8 * 1048576),
        )(*parts)

    tokens = P("pipe", "ctx", None)
    return jax.shard_map(
        body,
        mesh=mesh,
        in_specs=(tokens, tokens, tokens, tokens, P("pipe", None)),
        out_specs=(tokens, tokens, tokens, tokens),
        check_vma=False,
    )
```
